256 devices in a mesh: lat: 64 (over z, x, core), dep: 4 (over y).
Axes of the slice: x: 4, y: 4, z: 8, core: 2. Of those that a mesh axis runs over, the one named last changes fastest.
Arguments:
- kernel: bfloat16 [131072, 64, 128], P(('lat', 'dep')), may hold values from -0.1875 to 0.1875
- coefficient: float32 [131072, 256], P(('lat', 'dep')), may hold values from -3 to 3
- observed: float32 [16384, 64], P(('lat', 'dep')), may hold values from -6 to 6
- ray_brick: int32 [131072, 1], P(('lat', 'dep')), may hold values from 0 to 255; in each aligned block of 512 rows (0 to 511, 512 to 1023, ...) at most 3 rows name the same one
- tile_index: int32 [131072], P(('lat', 'dep')), may hold values from 0 to 511
- ray_count: int32 [256], P(('lat', 'dep')), may hold values from 32 to 64, as said below
- earth_model: float32 [256, 4, 512, 128], P(('lat', 'dep')), may hold values from -6 to 6
Outputs:
- residual: float32 [16384, 64], P(('lat', 'dep'))
- gradient: float32 [256, 4, 512, 128], P(('lat', 'dep'))
The draws below stay inside these ranges and needn't reach their ends.
Inputs may be any that keep to these rules, and one draw needn't show every extreme that they name: `ray_brick`: among the hits of one device no brick is named more than 3 times, a bound that some block reaches. `ray_count`: the largest count is exactly 64.
All inputs are finite; a program needn't handle non-finite values.
Results may differ from the reference program's by a relative error of at most 0.0037.
Values may be sent and summed in bfloat16 or wider, within the bound.
No kernel may reach another device: no remote copies, remote signals or barrier semaphores. Data moves between devices by JAX's collectives and lax.ppermute only.
A program may use at most 64 MiB of HBM per device.

```python
import math
import jax
import jax.numpy as jnp
import numpy as np
from jax import lax

PARAMS = 4
BANDS = 64
CELLS = 128
TILES = 512
HITS_RAY = 8
RAYS_DEV = 64
BRICKS = 256
HITS_DEV = 512
CAP = 3
RAYS = 16384
HITS = 131072


def draw_ray_count(key, part):
    counts_drawn = jax.random.randint(key, (BRICKS,), RAYS_DEV // 2, RAYS_DEV + 1)
    fullest = jax.random.randint(jax.random.fold_in(key, 7), (), 0, BRICKS)
    return jnp.where(jnp.arange(BRICKS) == fullest, RAYS_DEV, counts_drawn).astype(jnp.int32)


def place_ends(drawn, key, smallest, largest):
    shape = drawn.shape
    spot = [jax.random.randint(jax.random.fold_in(key, axis), (), 0, shape[axis]) for axis in range(len(shape))]
    drawn = drawn.at[tuple(spot)].set(smallest)
    longest = shape.index(max(shape))
    spot[longest] = (spot[longest] + 1) % shape[longest]
    return drawn.at[tuple(spot)].set(largest)


def block_scale(key, extent, shards, smallest, largest):
    def one(position, parts):
        steps = jax.random.uniform(jax.random.fold_in(jax.random.fold_in(key, 6), position), (parts,), jnp.float32, smallest / len(shards), largest / len(shards))
        return jnp.repeat(jnp.exp(steps), extent[position] // parts).reshape((-1,) + (1,) * (len(extent) - position - 1))

    loudness = one(*shards[0])
    for cut in shards[1:]:
        loudness = loudness * one(*cut)
    return loudness


def shared_out(key, own, number, rows, amount, top, bound, skew):
    ranking = jax.random.permutation(key, amount)
    crowded, common = shares(amount, rows * top, bound, skew, True), shares(amount, rows * top, bound, skew, False)
    places = jnp.arange(amount)

    def named(lengths, turn):
        used = int((lengths > 0).sum())
        fixed = max(1, used // 4)
        shifted = fixed + (places - fixed + turn * (used - fixed)) % max(1, amount - fixed)
        return jnp.zeros((amount,), jnp.int32).at[ranking[jnp.where(places < fixed, places, shifted)]].set(jnp.asarray(lengths, jnp.int32))

    lengths = jnp.where(number % 4 == 0, named(crowded, number // 4), named(common, number - number // 4 - 1))
    mixed = jax.random.permutation(jax.random.fold_in(own, 3), amount)
    donor, sink = mixed[0:amount // 2 * 2:2], mixed[1:amount // 2 * 2:2]
    margin = jnp.minimum(lengths[donor] - 1, bound - lengths[sink]) // 2
    margin = jnp.where((donor == ranking[0]) | (sink == ranking[0]) | (lengths[sink] == 0), 0, jnp.maximum(margin, 0))
    shifted = jax.random.randint(jax.random.fold_in(own, 4), (amount // 2,), 0, 1 << 20) % (margin + 1)
    lengths = lengths.at[donor].add(-shifted).at[sink].add(shifted)
    members = jnp.searchsorted(jnp.cumsum(lengths), jnp.arange(rows * top), side="right").astype(jnp.int32)
    grid = members.reshape(top, rows).T
    grid = grid[jax.random.permutation(jax.random.fold_in(own, 1), rows)]
    turn = jax.random.randint(jax.random.fold_in(own, 2), (rows, 1), 0, top)
    return jnp.take_along_axis(grid, (jnp.arange(top)[None, :] + turn) % top, axis=1)


def shares(count, total, reach, lean, full):
    portions = [(1 << 20) // math.isqrt(grade ** lean) + 1 for grade in range(1, count + 1)]
    largest = reach if full else min(reach, max(-(-total // count), total * portions[0] // sum(portions)))
    least = 1 if total - largest >= count - 1 else 0
    given, surplus = [largest] + [least] * (count - 1), total - largest - least * (count - 1)
    while surplus > 0:
        free = [i for i in range(1, count) if given[i] < largest] or [i for i in range(1, count) if given[i] < reach]
        mass, left = sum([portions[i] for i in free]), surplus
        for i in free:
            addition = min(reach - given[i], max(1, left * portions[i] // mass), surplus)
            given[i] = given[i] + addition
            surplus = surplus - addition
    return np.array(given)


def noise(rng, shape, width, limit, cuts=(), kind=jnp.bfloat16):
    array = jax.random.normal(rng, shape, jnp.float32) * width
    if len(cuts) > 0:
        array = block_scale(rng, shape, cuts, -0.22, 0.18) * array
    return jnp.clip(array, min=-limit, max=limit).astype(kind)


def setup_inputs(seed: int = 0) -> dict:
    keys = jax.random.split(jax.random.key(seed), 8)
    kernel = noise(keys[0], (HITS, BANDS, CELLS), (CELLS * HITS_RAY) ** -0.5, 0.1875, ((0, 256),))
    coefficient = noise(keys[1], (HITS, PARAMS * BANDS), PARAMS ** -0.5, 3.0, ((0, 256),), jnp.float32)
    observed = noise(keys[2], (RAYS, BANDS), 1.0, 6.0, ((0, 256),), jnp.float32)
    ray_brick_keys = jax.random.split(jax.random.fold_in(keys[3], 1), HITS // HITS_DEV)
    ray_brick_turns = jax.random.permutation(jax.random.fold_in(keys[3], 3), HITS // HITS_DEV)
    ray_brick = jax.vmap(lambda own, number: shared_out(jax.random.fold_in(keys[3], 2), own, number, HITS_DEV, BRICKS, 1, CAP, 2))(ray_brick_keys, ray_brick_turns).reshape((HITS, 1))
    tile_index = place_ends(jax.random.randint(keys[4], (HITS,), 0, TILES), jax.random.fold_in(keys[4], 1), 0, TILES - 1).astype(jnp.int32)
    ray_count = draw_ray_count(jax.random.fold_in(keys[7], 71), 0)
    earth_model = noise(keys[6], (BRICKS, PARAMS, TILES, CELLS), 1.0, 6.0, ((0, 256),), jnp.float32)
    return dict(kernel=kernel, coefficient=coefficient, observed=observed, ray_brick=ray_brick, tile_index=tile_index, ray_count=ray_count, earth_model=earth_model)


def reference(kernel, coefficient, observed, ray_brick, tile_index, ray_count, earth_model):
    model_low = lax.optimization_barrier(earth_model.astype(jnp.bfloat16))
    kernel_split = kernel.reshape(BRICKS, HITS_DEV, BANDS, CELLS)
    coefficient_split = coefficient.reshape(BRICKS, HITS_DEV, PARAMS, BANDS)
    observed_split = observed.reshape(BRICKS, RAYS_DEV, BANDS)
    brick_split = ray_brick.reshape(BRICKS, HITS_DEV).astype(jnp.int32)
    tile_split = tile_index.reshape(BRICKS, HITS_DEV).astype(jnp.int32)

    def advance(gradient, inputs):
        kernel_block, coefficient_block, observed_block, brick_block, tile_block, live_count = inputs
        block = model_low[brick_block, :, tile_block, :].astype(jnp.float32)
        kernel_wide = kernel_block.astype(jnp.float32)
        sensitivity = jnp.einsum("hbc,hpc->hpb", kernel_wide, block)
        contribution = jnp.sum(coefficient_block * sensitivity, axis=1)
        predicted = jnp.sum(contribution.reshape(RAYS_DEV, HITS_RAY, BANDS), axis=1)
        live_rays = jnp.arange(RAYS_DEV) < live_count
        residual = jnp.where(live_rays[:, None], predicted - observed_block, jnp.zeros_like(predicted))
        residual_hit = jnp.repeat(residual, HITS_RAY, axis=0)
        weight = lax.optimization_barrier((coefficient_block * residual_hit[:, None, :]).astype(jnp.bfloat16))
        gradient_term = jnp.einsum("hpb,hbc->hpc", weight.astype(jnp.float32), kernel_wide)
        gradient = gradient.at[brick_block, :, tile_block, :].add(gradient_term)
        return gradient, residual

    start = jnp.zeros(earth_model.shape, jnp.float32)
    gradient, residual = lax.scan(advance, start, (kernel_split, coefficient_split, observed_split, brick_split, tile_split, ray_count))
    return residual.reshape(RAYS, BANDS), gradient
```

```python
import functools

import jax
import jax.numpy as jnp
from jax import lax
from jax.experimental import pallas as pl
from jax.experimental.pallas import tpu as pltpu
from jax.sharding import PartitionSpec as P

SLOTS = 3
AXES = ("lat", "dep")
VMEM = pl.BlockSpec(memory_space=pltpu.VMEM)
SMEM = pl.BlockSpec(memory_space=pltpu.SMEM)
ANY = pl.BlockSpec(memory_space=pl.ANY)


def iota(shape, axis):
    return lax.broadcasted_iota(jnp.int32, shape, axis)


def column_of(row):
    wide = jnp.broadcast_to(row.astype(jnp.float32), (128, row.shape[1]))
    return wide.T


def plan_kernel(count_ref, brick_ref, tile_ref, wanted_ref, slot_ref, *, per_ray, devices):
    hits = brick_ref.shape[1]
    live = count_ref[0] * per_ray
    brick = brick_ref[...].astype(jnp.float32)
    down = column_of(brick)
    ranks = []
    for start in range(0, hits, 128):
        across = brick[:, start : start + 128]
        first = iota((hits, 128), 0)
        earlier = (down == across) & (first < iota((hits, 128), 1) + start) & (first < live)
        ranks.append(jnp.sum(earlier.astype(jnp.float32), axis=0, keepdims=True))
    rank = jnp.concatenate(ranks, axis=1)
    alive = iota((1, hits), 1) < live
    slot = jnp.where(alive, rank * devices + brick, -1.0)
    slot_ref[...] = slot
    tile = tile_ref[...].astype(jnp.float32) + 1.0
    owner = iota((devices, 1), 0).astype(jnp.float32)
    lane = iota((devices, 128), 1)
    wanted = jnp.zeros((devices, 128), jnp.float32)
    for k in range(SLOTS):
        hit = jnp.where(slot == owner + float(k * devices), tile, 0.0)
        wanted = jnp.where(lane == k, jnp.sum(hit, axis=1, keepdims=True), wanted)
    wanted_ref[...] = wanted.astype(jnp.int32)


def spread(product, spread_ref, k, rows, params, cells):
    for p in range(params):
        spread_ref[pl.ds(k * params + p, rows, stride=SLOTS * params), :] = product[:, p * cells : (p + 1) * cells]


def gathered(spread_ref, k, rows, params):
    parts = [spread_ref[pl.ds(k * params + p, rows, stride=SLOTS * params), :] for p in range(params)]
    return jnp.concatenate(parts, axis=1).astype(jnp.bfloat16)


def fetch_kernel(wanted_ref, model_ref, out_ref, spread_ref):
    params, tiles, cells = model_ref.shape
    devices = wanted_ref.shape[0]
    model = jnp.concatenate([model_ref[p].astype(jnp.bfloat16) for p in range(params)], axis=1)
    wanted = wanted_ref[...]
    for k in range(SLOTS):
        pick = wanted[:, k : k + 1] == iota((devices, tiles), 1) + 1
        pick = pick.astype(jnp.float32).astype(jnp.bfloat16)
        product = jnp.dot(pick, model, preferred_element_type=jnp.float32)
        spread(product, spread_ref, k, devices, params, cells)
    out_ref[...] = spread_ref[...].astype(jnp.bfloat16)


def rays_kernel(
    count_ref, slot_ref, arrived_ref, coefficient_ref, observed_ref, kernel_ref,
    residual_ref, out_ref, spread_ref, own_ref, grad_ref, held_ref, sems, *, per_ray, params, chunks, group,
):
    hits, bands, cells = held_ref.shape
    rays = observed_ref.shape[0]
    devices = arrived_ref.shape[0] // (SLOTS * params)
    step = hits // chunks
    copies = [
        pltpu.make_async_copy(kernel_ref.at[pl.ds(i * step, step)], held_ref.at[pl.ds(i * step, step)], sems.at[i])
        for i in range(chunks)
    ]
    for copy in copies:
        copy.start()
    spread_ref[...] = arrived_ref[...].astype(jnp.float32)
    slot = slot_ref[...]
    slot_down = column_of(slot)
    picks = []
    for start in range(0, SLOTS * devices, 128):
        pick = slot_down == (iota((hits, 128), 1) + start).astype(jnp.float32)
        picks.append(pick.astype(jnp.float32).astype(jnp.bfloat16))
    pick = jnp.concatenate(picks, axis=1)
    blocks = jnp.concatenate([gathered(spread_ref, k, devices, params) for k in range(SLOTS)], axis=0)
    own_ref[...] = jnp.dot(pick, blocks, preferred_element_type=jnp.float32)

    lane = iota((per_ray, 128), 1)
    low = lane < bands
    pairs = per_ray * bands // 128
    mine = [iota((per_ray, 128), 0) == 2 * j + lane // bands for j in range(pairs)]
    live = count_ref[0]

    def one(ray):
        rows = pl.ds(pl.multiple_of(ray * per_ray, per_ray), per_ray)
        block = jnp.concatenate([own_ref[rows, p * cells : (p + 1) * cells] for p in range(params)], axis=0)
        sheet = held_ref[rows].reshape(per_ray * bands, cells)
        sense = lax.dot_general(
            block.astype(jnp.bfloat16), sheet, (((1,), (1,)), ((), ())), preferred_element_type=jnp.float32
        )
        scale = []
        for half in range(params // 2):
            two = coefficient_ref[rows, half * 128 : half * 128 + 128]
            turned = pltpu.roll(two, bands, 1)
            scale.append(jnp.where(low, two, turned))
            scale.append(jnp.where(low, turned, two))
        total = jnp.zeros((per_ray, 128), jnp.float32)
        for j in range(pairs):
            part = jnp.zeros((per_ray, 128), jnp.float32)
            for p in range(params):
                part += scale[p] * sense[p * per_ray : (p + 1) * per_ray, j * 128 : (j + 1) * 128]
            total += jnp.where(mine[j], part, 0.0)
        predicted = jnp.sum(total, axis=0, keepdims=True)
        predicted = predicted + pltpu.roll(predicted, bands, 1)
        seen = observed_ref[pl.ds(ray, 1), :]
        residual = jnp.where(ray < live, predicted - jnp.concatenate([seen, seen], axis=1), 0.0)
        residual_ref[pl.ds(ray, 1), :] = residual[:, :bands]
        weights = [p * residual for p in scale]
        weight = jnp.concatenate(
            [jnp.concatenate([jnp.where(mine[j], w, 0.0) for j in range(pairs)], axis=1) for w in weights], axis=0
        ).astype(jnp.bfloat16)
        term = jnp.dot(weight, sheet, preferred_element_type=jnp.float32)
        for p in range(params):
            grad_ref[rows, p * cells : (p + 1) * cells] = term[p * per_ray : (p + 1) * per_ray]

    rays_step = step // per_ray
    for i in range(chunks):
        copies[i].wait()

        def several(g, carry, i=i):
            for n in range(group):
                one(i * rays_step + g * group + n)
            return carry

        lax.fori_loop(0, rays_step // group, several, 0)

    grad = grad_ref[...].astype(jnp.bfloat16)
    for k in range(SLOTS):
        place = slot == (iota((devices, hits), 0) + k * devices).astype(jnp.float32)
        place = place.astype(jnp.float32).astype(jnp.bfloat16)
        product = jnp.dot(place, grad, preferred_element_type=jnp.float32)
        spread(product, spread_ref, k, devices, params, cells)
    out_ref[...] = spread_ref[...].astype(jnp.bfloat16)


def sum_kernel(wanted_ref, returned_ref, out_ref, spread_ref):
    params, tiles, cells = out_ref.shape
    devices = wanted_ref.shape[0]
    spread_ref[...] = returned_ref[...].astype(jnp.float32)
    across = wanted_ref[...].astype(jnp.float32).T
    picks = []
    for k in range(SLOTS):
        pick = across[k : k + 1, :] == (iota((tiles, devices), 0) + 1).astype(jnp.float32)
        picks.append(pick.astype(jnp.float32).astype(jnp.bfloat16))
    pick = jnp.concatenate(picks, axis=1)
    blocks = jnp.concatenate([gathered(spread_ref, k, devices, params) for k in range(SLOTS)], axis=0)
    for p in range(params):
        out_ref[p] = jnp.dot(pick, blocks[:, p * cells : (p + 1) * cells], preferred_element_type=jnp.float32)


def exchange(rows, devices, params, cells):
    sent = rows.reshape(devices, SLOTS, params, cells)
    back = lax.all_to_all(sent, AXES, split_axis=0, concat_axis=0, tiled=True)
    return back.reshape(devices * SLOTS * params, cells)


def per_device(kernel, coefficient, observed, ray_brick, tile_index, ray_count, earth_model):
    hits, bands, cells = kernel.shape
    params, tiles = earth_model.shape[1:3]
    rays = observed.shape[0]
    per_ray = hits // rays
    devices = lax.axis_size("lat") * lax.axis_size("dep")
    messages = devices * SLOTS * params
    f32, bf16 = jnp.float32, jnp.bfloat16
    shape = jax.ShapeDtypeStruct

    wanted, slot = pl.pallas_call(
        functools.partial(plan_kernel, per_ray=per_ray, devices=devices),
        out_shape=(shape((devices, 128), jnp.int32), shape((1, hits), f32)),
        in_specs=[SMEM, VMEM, VMEM],
        out_specs=(VMEM, VMEM),
        name="plan",
    )(ray_count, ray_brick.reshape(1, hits), tile_index.reshape(1, hits))
    requests = lax.all_to_all(wanted.reshape(devices, 1, 128), AXES, split_axis=0, concat_axis=0, tiled=True)
    requests = requests.reshape(devices, 128)
    blocks = pl.pallas_call(
        fetch_kernel,
        out_shape=shape((messages, cells), bf16),
        in_specs=[VMEM, VMEM],
        out_specs=VMEM,
        scratch_shapes=[pltpu.VMEM((messages, cells), f32)],
        name="fetch",
    )(requests, earth_model[0])
    arrived = exchange(blocks, devices, params, cells)
    chunks = 8
    residual, outgoing = pl.pallas_call(
        functools.partial(rays_kernel, per_ray=per_ray, params=params, chunks=chunks, group=8),
        out_shape=(shape((rays, bands), f32), shape((messages, cells), bf16)),
        in_specs=[SMEM, VMEM, VMEM, VMEM, VMEM, ANY],
        out_specs=(VMEM, VMEM),
        scratch_shapes=[
            pltpu.VMEM((messages, cells), f32),
            pltpu.VMEM((hits, params * cells), f32),
            pltpu.VMEM((hits, params * cells), f32),
            pltpu.VMEM((hits, bands, cells), bf16),
            pltpu.SemaphoreType.DMA((chunks,)),
        ],
        name="rays",
    )(ray_count, slot, arrived, coefficient, observed, kernel)
    returned = exchange(outgoing, devices, params, cells)
    gradient = pl.pallas_call(
        sum_kernel,
        out_shape=shape((params, tiles, cells), f32),
        in_specs=[VMEM, VMEM],
        out_specs=VMEM,
        scratch_shapes=[pltpu.VMEM((messages, cells), f32)],
        name="add",
    )(requests, returned)
    return residual, gradient[None]


def solution(mesh):
    return jax.shard_map(
        per_device,
        mesh=mesh,
        in_specs=(
            P(AXES, None, None),
            P(AXES, None),
            P(AXES, None),
            P(AXES, None),
            P(AXES),
            P(AXES),
            P(AXES, None, None, None),
        ),
        out_specs=(P(AXES, None), P(AXES, None, None, None)),
        check_vma=False,
    )
```

```python
import functools

import jax
import jax.numpy as jnp
from jax import lax
from jax.experimental import pallas as pl
from jax.experimental.pallas import tpu as pltpu
from jax.sharding import PartitionSpec as P

SLOTS = 3
MIB = 1 << 20
AXES = ("lat", "dep")
VMEM = pl.BlockSpec(memory_space=pltpu.VMEM)
SMEM = pl.BlockSpec(memory_space=pltpu.SMEM)
HBM = pl.BlockSpec(memory_space=pltpu.HBM)


def in_hbm(array):
    return pltpu.with_memory_space_constraint(array, pltpu.HBM)


def iota(shape, axis):
    return lax.broadcasted_iota(jnp.int32, shape, axis)


def column_of(row):
    wide = jnp.broadcast_to(row.astype(jnp.float32), (128, row.shape[1]))
    return wide.T


def plan_kernel(
    count_ref, brick_hbm, tile_hbm, wanted_ref, slot_ref, brick_ref, tile_ref, sems, *, per_ray, devices
):
    brick_copy = pltpu.make_async_copy(brick_hbm, brick_ref, sems.at[0])
    tile_copy = pltpu.make_async_copy(tile_hbm, tile_ref, sems.at[1])
    brick_copy.start()
    tile_copy.start()
    hits = brick_ref.shape[1]
    live = count_ref[0] * per_ray
    brick_copy.wait()
    tile_copy.wait()
    brick = brick_ref[...].astype(jnp.float32)
    down = column_of(brick)
    ranks = []
    for start in range(0, hits, 128):
        across = brick[:, start : start + 128]
        first = iota((hits, 128), 0)
        earlier = (down == across) & (first < iota((hits, 128), 1) + start) & (first < live)
        ranks.append(jnp.sum(earlier.astype(jnp.float32), axis=0, keepdims=True))
    rank = jnp.concatenate(ranks, axis=1)
    alive = iota((1, hits), 1) < live
    slot = jnp.where(alive, rank * devices + brick, -1.0)
    slot_ref[...] = slot
    tile = tile_ref[...].astype(jnp.float32) + 1.0
    owner = iota((devices, 1), 0).astype(jnp.float32)
    lane = iota((devices, 128), 1)
    wanted = jnp.zeros((devices, 128), jnp.float32)
    for k in range(SLOTS):
        hit = jnp.where(slot == owner + float(k * devices), tile, 0.0)
        wanted = jnp.where(lane == k, jnp.sum(hit, axis=1, keepdims=True), wanted)
    wanted_ref[...] = wanted.astype(jnp.int32)


def spread(product, spread_ref, k, rows, params, cells):
    for p in range(params):
        spread_ref[pl.ds(k * params + p, rows, stride=SLOTS * params), :] = product[:, p * cells : (p + 1) * cells]


def gathered(spread_ref, k, rows, params):
    parts = [spread_ref[pl.ds(k * params + p, rows, stride=SLOTS * params), :] for p in range(params)]
    return jnp.concatenate(parts, axis=1).astype(jnp.bfloat16)


def round_kernel(model_ref, low_ref):
    params, _, cells = model_ref.shape
    for p in range(params):
        low_ref[:, p * cells : (p + 1) * cells] = model_ref[p].astype(jnp.bfloat16)


def fetch_kernel(wanted_ref, model_ref, out_ref, spread_ref, *, params):
    tiles = model_ref.shape[0]
    cells = model_ref.shape[1] // params
    devices = wanted_ref.shape[0]
    model = model_ref[...]
    wanted = wanted_ref[...]
    for k in range(SLOTS):
        pick = wanted[:, k : k + 1] == iota((devices, tiles), 1) + 1
        pick = pick.astype(jnp.float32).astype(jnp.bfloat16)
        product = jnp.dot(pick, model, preferred_element_type=jnp.float32)
        spread(product, spread_ref, k, devices, params, cells)
    out_ref[...] = spread_ref[...].astype(jnp.bfloat16)


def rays_kernel(
    count_ref, slot_ref, arrived_ref, coefficient_hbm, observed_hbm, kernel_ref,
    residual_ref, out_ref, coefficient_ref, observed_ref, spread_ref, own_ref, grad_ref, total_ref, twice_ref,
    held_ref, sems, small_sems,
    *, per_ray, params, group,
):
    hits, bands, cells = held_ref.shape
    rays = observed_ref.shape[0]
    devices = arrived_ref.shape[0] // (SLOTS * params)
    chunks = rays // group
    step = group * per_ray

    def fetch(i):
        part = pl.ds(i * step, step)
        return pltpu.make_async_copy(kernel_ref.at[part], held_ref.at[part], sems.at[i])

    coefficient_copy = pltpu.make_async_copy(coefficient_hbm, coefficient_ref, small_sems.at[0])
    observed_copy = pltpu.make_async_copy(observed_hbm, observed_ref, small_sems.at[1])
    coefficient_copy.start()
    for i in range(chunks):
        fetch(i).start()
    observed_copy.start()
    spread_ref[...] = arrived_ref[...].astype(jnp.float32)
    slot = slot_ref[...]
    slot_down = column_of(slot)
    picks = []
    for start in range(0, SLOTS * devices, 128):
        pick = slot_down == (iota((hits, 128), 1) + start).astype(jnp.float32)
        picks.append(pick.astype(jnp.float32).astype(jnp.bfloat16))
    pick = jnp.concatenate(picks, axis=1)
    blocks = jnp.concatenate([gathered(spread_ref, k, devices, params) for k in range(SLOTS)], axis=0)
    for p in range(params):
        own = jnp.dot(pick, blocks[:, p * cells : (p + 1) * cells], preferred_element_type=jnp.float32)
        own_ref[:, p * per_ray : (p + 1) * per_ray, :] = own.reshape(rays, per_ray, cells)

    lane = iota((per_ray, 128), 1)
    low = lane < bands
    pairs = per_ray * bands // 128
    mine = [iota((per_ray, 128), 0) == 2 * j + lane // bands for j in range(pairs)]

    def scales(rows):
        scale = []
        for half in range(params // 2):
            two = coefficient_ref[rows, half * 128 : half * 128 + 128]
            turned = pltpu.roll(two, bands, 1)
            scale.append(jnp.where(low, two, turned))
            scale.append(jnp.where(low, turned, two))
        return scale

    def rows_of(ray):
        return pl.ds(pl.multiple_of(ray * per_ray, per_ray), per_ray)

    def sense(ray):
        rows = rows_of(ray)
        sheet = held_ref[rows].reshape(per_ray * bands, cells)
        sensed = lax.dot_general(
            own_ref[ray].astype(jnp.bfloat16), sheet, (((1,), (1,)), ((), ())), preferred_element_type=jnp.float32
        )
        scale = scales(rows)
        total = jnp.zeros((per_ray, 128), jnp.float32)
        for j in range(pairs):
            part = scale[0] * sensed[:per_ray, j * 128 : (j + 1) * 128]
            for p in range(1, params):
                part += scale[p] * sensed[p * per_ray : (p + 1) * per_ray, j * 128 : (j + 1) * 128]
            total = jnp.where(mine[j], part, total)
        total_ref[rows, :] = total

    coefficient_copy.wait()

    def forward(g, carry):
        fetch(g).wait()
        for n in range(group):
            sense(g * group + n)
        return carry

    lax.fori_loop(0, chunks, forward, 0)

    predicted = total_ref[pl.ds(0, rays, stride=per_ray), :]
    for i in range(1, per_ray):
        predicted += total_ref[pl.ds(i, rays, stride=per_ray), :]
    predicted = predicted + pltpu.roll(predicted, bands, 1)
    observed_copy.wait()
    seen = observed_ref[...]
    seen = jnp.concatenate([seen, seen], axis=1)
    residual = jnp.where(iota((rays, 128), 0) < count_ref[0], predicted - seen, 0.0)
    residual_ref[...] = residual[:, :bands]
    twice_ref[...] = residual

    rows_all = params * per_ray
    keep = [
        (iota((rows_all, 128), 0) % per_ray == 2 * j + iota((rows_all, 128), 1) // bands)
        .astype(jnp.float32)
        .astype(jnp.bfloat16)
        for j in range(pairs)
    ]

    def adjoint(ray):
        rows = rows_of(ray)
        sheet = held_ref[rows].reshape(per_ray * bands, cells)
        residual = twice_ref[pl.ds(ray, 1), :]
        weight = jnp.concatenate([p * residual for p in scales(rows)], axis=0).astype(jnp.bfloat16)
        weight = jnp.concatenate([weight * keep[j] for j in range(pairs)], axis=1)
        grad_ref[ray] = jnp.dot(weight, sheet, preferred_element_type=jnp.float32)

    def backward(g, carry):
        for n in range(group):
            adjoint(g * group + n)
        return carry

    lax.fori_loop(0, chunks, backward, 0)

    grad = jnp.concatenate(
        [grad_ref[:, p * per_ray : (p + 1) * per_ray, :].reshape(hits, cells) for p in range(params)], axis=1
    ).astype(jnp.bfloat16)
    for k in range(SLOTS):
        place = slot == (iota((devices, hits), 0) + k * devices).astype(jnp.float32)
        place = place.astype(jnp.float32).astype(jnp.bfloat16)
        product = jnp.dot(place, grad, preferred_element_type=jnp.float32)
        spread(product, spread_ref, k, devices, params, cells)
    out_ref[...] = spread_ref[...].astype(jnp.bfloat16)


def sum_kernel(wanted_ref, returned_ref, out_hbm, spread_ref, out_ref, sems):
    params, tiles, cells = out_ref.shape
    devices = wanted_ref.shape[0]
    spread_ref[...] = returned_ref[...].astype(jnp.float32)
    across = wanted_ref[...].astype(jnp.float32).T
    picks = []
    for k in range(SLOTS):
        pick = across[k : k + 1, :] == (iota((tiles, devices), 0) + 1).astype(jnp.float32)
        picks.append(pick.astype(jnp.float32).astype(jnp.bfloat16))
    pick = jnp.concatenate(picks, axis=1)
    blocks = jnp.concatenate([gathered(spread_ref, k, devices, params) for k in range(SLOTS)], axis=0)
    for p in range(params):
        out_ref[p] = jnp.dot(pick, blocks[:, p * cells : (p + 1) * cells], preferred_element_type=jnp.float32)
        pltpu.make_async_copy(out_ref.at[p], out_hbm.at[p], sems.at[p]).start()
    for p in range(params):
        pltpu.make_async_copy(out_ref.at[p], out_hbm.at[p], sems.at[p]).wait()


def exchange(rows, devices, params, cells):
    sent = rows.reshape(devices, SLOTS, params, cells)
    back = lax.all_to_all(sent, AXES, split_axis=0, concat_axis=0, tiled=True)
    return back.reshape(devices * SLOTS * params, cells)


def per_device(kernel, coefficient, observed, ray_brick, tile_index, ray_count, earth_model):
    hits, bands, cells = kernel.shape
    params, tiles = earth_model.shape[1:3]
    rays = observed.shape[0]
    per_ray = hits // rays
    devices = lax.axis_size("lat") * lax.axis_size("dep")
    messages = devices * SLOTS * params
    f32, bf16 = jnp.float32, jnp.bfloat16
    shape = jax.ShapeDtypeStruct

    wanted, slot = pl.pallas_call(
        functools.partial(plan_kernel, per_ray=per_ray, devices=devices),
        out_shape=(shape((devices, 128), jnp.int32), shape((1, hits), f32)),
        in_specs=[SMEM, HBM, HBM],
        out_specs=(VMEM, VMEM),
        scratch_shapes=[
            pltpu.VMEM((1, hits), jnp.int32),
            pltpu.VMEM((1, hits), jnp.int32),
            pltpu.SemaphoreType.DMA((2,)),
        ],
        compiler_params=pltpu.CompilerParams(vmem_limit_bytes=8 * MIB),
        name="plan",
    )(ray_count, in_hbm(ray_brick.reshape(1, hits)), in_hbm(tile_index.reshape(1, hits)))
    requests = lax.all_to_all(wanted.reshape(devices, 1, 128), AXES, split_axis=0, concat_axis=0, tiled=True)
    requests = requests.reshape(devices, 128)
    model = pl.pallas_call(
        round_kernel,
        out_shape=shape((tiles, params * cells), bf16),
        in_specs=[VMEM],
        out_specs=VMEM,
        compiler_params=pltpu.CompilerParams(vmem_limit_bytes=8 * MIB),
        cost_estimate=pl.CostEstimate(flops=0, bytes_accessed=6 * tiles * params * cells, transcendentals=0),
        name="round",
    )(in_hbm(earth_model[0]))
    blocks = pl.pallas_call(
        functools.partial(fetch_kernel, params=params),
        out_shape=shape((messages, cells), bf16),
        in_specs=[VMEM, VMEM],
        out_specs=VMEM,
        scratch_shapes=[pltpu.VMEM((messages, cells), f32)],
        compiler_params=pltpu.CompilerParams(vmem_limit_bytes=16 * MIB),
        name="fetch",
    )(requests, model)
    arrived = exchange(blocks, devices, params, cells)
    group = 16
    residual, outgoing = pl.pallas_call(
        functools.partial(rays_kernel, per_ray=per_ray, params=params, group=group),
        out_shape=(shape((rays, bands), f32), shape((messages, cells), bf16)),
        in_specs=[SMEM, VMEM, VMEM, HBM, HBM, HBM],
        out_specs=(VMEM, VMEM),
        scratch_shapes=[
            pltpu.VMEM((hits, params * bands), f32),
            pltpu.VMEM((rays, bands), f32),
            pltpu.VMEM((messages, cells), f32),
            pltpu.VMEM((rays, params * per_ray, cells), f32),
            pltpu.VMEM((rays, params * per_ray, cells), f32),
            pltpu.VMEM((hits, 128), f32),
            pltpu.VMEM((rays, 128), f32),
            pltpu.VMEM((hits, bands, cells), bf16),
            pltpu.SemaphoreType.DMA((rays // group,)),
            pltpu.SemaphoreType.DMA((2,)),
        ],
        compiler_params=pltpu.CompilerParams(vmem_limit_bytes=28 * MIB),
        name="rays",
    )(ray_count, slot, arrived, in_hbm(coefficient), in_hbm(observed), in_hbm(kernel))
    returned = exchange(outgoing, devices, params, cells)
    gradient = pl.pallas_call(
        sum_kernel,
        out_shape=shape((params, tiles, cells), f32),
        in_specs=[VMEM, VMEM],
        out_specs=HBM,
        scratch_shapes=[
            pltpu.VMEM((messages, cells), f32),
            pltpu.VMEM((params, tiles, cells), f32),
            pltpu.SemaphoreType.DMA((params,)),
        ],
        compiler_params=pltpu.CompilerParams(vmem_limit_bytes=16 * MIB),
        name="add",
    )(requests, returned)
    return residual, gradient[None]


def solution(mesh):
    return jax.shard_map(
        per_device,
        mesh=mesh,
        in_specs=(
            P(AXES, None, None),
            P(AXES, None),
            P(AXES, None),
            P(AXES, None),
            P(AXES),
            P(AXES),
            P(AXES, None, None, None),
        ),
        out_specs=(P(AXES, None), P(AXES, None, None, None)),
        check_vma=False,
    )
```

```python
import functools

import jax
import jax.numpy as jnp
from jax import lax
from jax.experimental import pallas as pl
from jax.experimental.pallas import tpu as pltpu
from jax.sharding import PartitionSpec as P

SLOTS = 3
MIB = 1 << 20
AXES = ("lat", "dep")
VMEM = pl.BlockSpec(memory_space=pltpu.VMEM)
SMEM = pl.BlockSpec(memory_space=pltpu.SMEM)
HBM = pl.BlockSpec(memory_space=pltpu.HBM)


def in_hbm(array):
    return pltpu.with_memory_space_constraint(array, pltpu.HBM)


def iota(shape, axis):
    return lax.broadcasted_iota(jnp.int32, shape, axis)


def column_of(row):
    wide = jnp.broadcast_to(row.astype(jnp.float32), (128, row.shape[1]))
    return wide.T


def plan_kernel(
    count_ref, brick_hbm, tile_hbm, model_hbm, wanted_ref, slot_ref, low_ref, brick_ref, tile_ref, model_ref, sems,
    *, per_ray, devices,
):
    brick_copy = pltpu.make_async_copy(brick_hbm, brick_ref, sems.at[0])
    tile_copy = pltpu.make_async_copy(tile_hbm, tile_ref, sems.at[1])
    brick_copy.start()
    tile_copy.start()
    params, _, cells = model_ref.shape
    for p in range(params):
        pltpu.make_async_copy(model_hbm.at[p], model_ref.at[p], sems.at[2 + p]).start()
    hits = brick_ref.shape[1]
    live = count_ref[0] * per_ray
    brick_copy.wait()
    tile_copy.wait()
    brick = brick_ref[...].astype(jnp.float32)
    down = column_of(brick)
    ranks = []
    for start in range(0, hits, 128):
        across = brick[:, start : start + 128]
        first = iota((hits, 128), 0)
        earlier = (down == across) & (first < iota((hits, 128), 1) + start) & (first < live)
        ranks.append(jnp.sum(earlier.astype(jnp.float32), axis=0, keepdims=True))
    rank = jnp.concatenate(ranks, axis=1)
    alive = iota((1, hits), 1) < live
    slot = jnp.where(alive, rank * devices + brick, -1.0)
    slot_ref[...] = slot
    tile = tile_ref[...].astype(jnp.float32) + 1.0
    owner = iota((devices, 1), 0).astype(jnp.float32)
    lane = iota((devices, 128), 1)
    wanted = jnp.zeros((devices, 128), jnp.float32)
    for k in range(SLOTS):
        hit = jnp.where(slot == owner + float(k * devices), tile, 0.0)
        wanted = jnp.where(lane == k, jnp.sum(hit, axis=1, keepdims=True), wanted)
    wanted_ref[...] = wanted.astype(jnp.int32)
    for p in range(params):
        pltpu.make_async_copy(model_hbm.at[p], model_ref.at[p], sems.at[2 + p]).wait()
        low_ref[:, p * cells : (p + 1) * cells] = model_ref[p].astype(jnp.bfloat16)


def spread(product, spread_ref, rows, params, cells):
    for k in range(SLOTS):
        for p in range(params):
            part = product[k * rows : (k + 1) * rows, p * cells : (p + 1) * cells]
            spread_ref[pl.ds(k * params + p, rows, stride=SLOTS * params), :] = part


def gathered(spread_ref, k, rows, params):
    parts = [spread_ref[pl.ds(k * params + p, rows, stride=SLOTS * params), :] for p in range(params)]
    return jnp.concatenate(parts, axis=1).astype(jnp.bfloat16)


def fetch_kernel(wanted_ref, model_ref, out_ref, spread_ref, *, params):
    tiles = model_ref.shape[0]
    cells = model_ref.shape[1] // params
    devices = wanted_ref.shape[0]
    model = model_ref[...]
    wanted = wanted_ref[...]
    picks = []
    for k in range(SLOTS):
        pick = wanted[:, k : k + 1] == iota((devices, tiles), 1) + 1
        picks.append(pick.astype(jnp.float32).astype(jnp.bfloat16))
    pick = jnp.concatenate(picks, axis=0)
    spread(jnp.dot(pick, model, preferred_element_type=jnp.float32), spread_ref, devices, params, cells)
    out_ref[...] = spread_ref[...].astype(jnp.bfloat16)


def rays_kernel(
    count_ref, slot_ref, arrived_ref, coefficient_hbm, observed_hbm, kernel_ref,
    residual_ref, out_ref, coefficient_ref, observed_ref, spread_ref, own_ref, grad_ref, total_ref, twice_ref,
    held_ref, sems, small_sems,
    *, per_ray, params, group,
):
    hits, bands, cells = held_ref.shape
    rays = observed_ref.shape[0]
    devices = arrived_ref.shape[0] // (SLOTS * params)
    chunks = rays // group
    step = group * per_ray

    def fetch(i):
        part = pl.ds(i * step, step)
        return pltpu.make_async_copy(kernel_ref.at[part], held_ref.at[part], sems.at[i])

    coefficient_copy = pltpu.make_async_copy(coefficient_hbm, coefficient_ref, small_sems.at[0])
    observed_copy = pltpu.make_async_copy(observed_hbm, observed_ref, small_sems.at[1])
    coefficient_copy.start()
    for i in range(chunks):
        fetch(i).start()
    observed_copy.start()
    spread_ref[...] = arrived_ref[...].astype(jnp.float32)
    slot = slot_ref[...]
    slot_down = column_of(slot)
    picks = []
    for start in range(0, SLOTS * devices, 128):
        pick = slot_down == (iota((hits, 128), 1) + start).astype(jnp.float32)
        picks.append(pick.astype(jnp.float32).astype(jnp.bfloat16))
    pick = jnp.concatenate(picks, axis=1)
    blocks = jnp.concatenate([gathered(spread_ref, k, devices, params) for k in range(SLOTS)], axis=0)
    for p in range(0, params, 2):
        own = jnp.dot(pick, blocks[:, p * cells : (p + 2) * cells], preferred_element_type=jnp.float32)
        for q in range(2):
            part = own[:, q * cells : (q + 1) * cells].reshape(rays, per_ray, cells)
            own_ref[:, (p + q) * per_ray : (p + q + 1) * per_ray, :] = part

    lane = iota((per_ray, 128), 1)
    low = lane < bands
    pairs = per_ray * bands // 128
    mine = [iota((per_ray, 128), 0) == 2 * j + lane // bands for j in range(pairs)]

    def scales(rows):
        scale = []
        for half in range(params // 2):
            two = coefficient_ref[rows, half * 128 : half * 128 + 128]
            turned = pltpu.roll(two, bands, 1)
            scale.append(jnp.where(low, two, turned))
            scale.append(jnp.where(low, turned, two))
        return scale

    def rows_of(ray):
        return pl.ds(pl.multiple_of(ray * per_ray, per_ray), per_ray)

    def sense(ray):
        rows = rows_of(ray)
        sheet = held_ref[rows].reshape(per_ray * bands, cells)
        sensed = lax.dot_general(
            own_ref[ray].astype(jnp.bfloat16), sheet, (((1,), (1,)), ((), ())), preferred_element_type=jnp.float32
        )
        scale = scales(rows)
        total = jnp.zeros((per_ray, 128), jnp.float32)
        for j in range(pairs):
            part = scale[0] * sensed[:per_ray, j * 128 : (j + 1) * 128]
            for p in range(1, params):
                part += scale[p] * sensed[p * per_ray : (p + 1) * per_ray, j * 128 : (j + 1) * 128]
            total = jnp.where(mine[j], part, total)
        total_ref[rows, :] = total

    coefficient_copy.wait()

    def forward(g, carry):
        fetch(g).wait()
        for n in range(group):
            sense(g * group + n)
        return carry

    lax.fori_loop(0, chunks, forward, 0)

    predicted = total_ref[pl.ds(0, rays, stride=per_ray), :]
    for i in range(1, per_ray):
        predicted += total_ref[pl.ds(i, rays, stride=per_ray), :]
    predicted = predicted + pltpu.roll(predicted, bands, 1)
    observed_copy.wait()
    seen = observed_ref[...]
    seen = jnp.concatenate([seen, seen], axis=1)
    residual = jnp.where(iota((rays, 128), 0) < count_ref[0], predicted - seen, 0.0)
    residual_ref[...] = residual[:, :bands]
    twice_ref[...] = residual

    rows_all = params * per_ray
    keep = [
        (iota((rows_all, 128), 0) % per_ray == 2 * j + iota((rows_all, 128), 1) // bands)
        .astype(jnp.float32)
        .astype(jnp.bfloat16)
        for j in range(pairs)
    ]

    def adjoint(ray):
        rows = rows_of(ray)
        sheet = held_ref[rows].reshape(per_ray * bands, cells)
        residual = twice_ref[pl.ds(ray, 1), :]
        weight = jnp.concatenate([p * residual for p in scales(rows)], axis=0).astype(jnp.bfloat16)
        weight = jnp.concatenate([weight * keep[j] for j in range(pairs)], axis=1)
        grad_ref[ray] = jnp.dot(weight, sheet, preferred_element_type=jnp.float32)

    for n in range(rays):
        adjoint(n)

    grad = jnp.concatenate(
        [grad_ref[:, p * per_ray : (p + 1) * per_ray, :].reshape(hits, cells) for p in range(params)], axis=1
    ).astype(jnp.bfloat16)
    place = slot == iota((SLOTS * devices, hits), 0).astype(jnp.float32)
    place = place.astype(jnp.float32).astype(jnp.bfloat16)
    spread(jnp.dot(place, grad, preferred_element_type=jnp.float32), spread_ref, devices, params, cells)
    out_ref[...] = spread_ref[...].astype(jnp.bfloat16)


def sum_kernel(wanted_ref, returned_ref, out_hbm, spread_ref, out_ref, sems):
    params, tiles, cells = out_ref.shape
    devices = wanted_ref.shape[0]
    spread_ref[...] = returned_ref[...].astype(jnp.float32)
    across = wanted_ref[...].astype(jnp.float32).T
    picks = []
    for k in range(SLOTS):
        pick = across[k : k + 1, :] == (iota((tiles, devices), 0) + 1).astype(jnp.float32)
        picks.append(pick.astype(jnp.float32).astype(jnp.bfloat16))
    pick = jnp.concatenate(picks, axis=1)
    blocks = jnp.concatenate([gathered(spread_ref, k, devices, params) for k in range(SLOTS)], axis=0)
    for p in range(0, params, 2):
        total = jnp.dot(pick, blocks[:, p * cells : (p + 2) * cells], preferred_element_type=jnp.float32)
        for q in range(2):
            out_ref[p + q] = total[:, q * cells : (q + 1) * cells]
            pltpu.make_async_copy(out_ref.at[p + q], out_hbm.at[p + q], sems.at[p + q]).start()
    for p in range(params):
        pltpu.make_async_copy(out_ref.at[p], out_hbm.at[p], sems.at[p]).wait()


def exchange(rows, devices, params, cells):
    sent = rows.reshape(devices, SLOTS, params, cells)
    back = lax.all_to_all(sent, AXES, split_axis=0, concat_axis=0, tiled=True)
    return back.reshape(devices * SLOTS * params, cells)


def per_device(kernel, coefficient, observed, ray_brick, tile_index, ray_count, earth_model):
    hits, bands, cells = kernel.shape
    params, tiles = earth_model.shape[1:3]
    rays = observed.shape[0]
    per_ray = hits // rays
    devices = lax.axis_size("lat") * lax.axis_size("dep")
    messages = devices * SLOTS * params
    f32, bf16 = jnp.float32, jnp.bfloat16
    shape = jax.ShapeDtypeStruct

    wanted, slot, model = pl.pallas_call(
        functools.partial(plan_kernel, per_ray=per_ray, devices=devices),
        out_shape=(
            shape((devices, 128), jnp.int32),
            shape((1, hits), f32),
            shape((tiles, params * cells), bf16),
        ),
        in_specs=[SMEM, HBM, HBM, HBM],
        out_specs=(VMEM, VMEM, VMEM),
        scratch_shapes=[
            pltpu.VMEM((1, hits), jnp.int32),
            pltpu.VMEM((1, hits), jnp.int32),
            pltpu.VMEM((params, tiles, cells), f32),
            pltpu.SemaphoreType.DMA((2 + params,)),
        ],
        compiler_params=pltpu.CompilerParams(vmem_limit_bytes=8 * MIB),
        name="plan",
    )(ray_count, in_hbm(ray_brick.reshape(1, hits)), in_hbm(tile_index.reshape(1, hits)), in_hbm(earth_model[0]))
    requests = lax.all_to_all(wanted.reshape(devices, 1, 128), AXES, split_axis=0, concat_axis=0, tiled=True)
    requests = requests.reshape(devices, 128)
    blocks = pl.pallas_call(
        functools.partial(fetch_kernel, params=params),
        out_shape=shape((messages, cells), bf16),
        in_specs=[VMEM, VMEM],
        out_specs=VMEM,
        scratch_shapes=[pltpu.VMEM((messages, cells), f32)],
        compiler_params=pltpu.CompilerParams(vmem_limit_bytes=16 * MIB),
        name="fetch",
    )(requests, model)
    arrived = exchange(blocks, devices, params, cells)
    group = 16
    residual, outgoing = pl.pallas_call(
        functools.partial(rays_kernel, per_ray=per_ray, params=params, group=group),
        out_shape=(shape((rays, bands), f32), shape((messages, cells), bf16)),
        in_specs=[SMEM, VMEM, VMEM, HBM, HBM, HBM],
        out_specs=(VMEM, VMEM),
        scratch_shapes=[
            pltpu.VMEM((hits, params * bands), f32),
            pltpu.VMEM((rays, bands), f32),
            pltpu.VMEM((messages, cells), f32),
            pltpu.VMEM((rays, params * per_ray, cells), f32),
            pltpu.VMEM((rays, params * per_ray, cells), f32),
            pltpu.VMEM((hits, 128), f32),
            pltpu.VMEM((rays, 128), f32),
            pltpu.VMEM((hits, bands, cells), bf16),
            pltpu.SemaphoreType.DMA((rays // group,)),
            pltpu.SemaphoreType.DMA((2,)),
        ],
        compiler_params=pltpu.CompilerParams(vmem_limit_bytes=28 * MIB),
        name="rays",
    )(ray_count, slot, arrived, in_hbm(coefficient), in_hbm(observed), in_hbm(kernel))
    returned = exchange(outgoing, devices, params, cells)
    gradient = pl.pallas_call(
        sum_kernel,
        out_shape=shape((params, tiles, cells), f32),
        in_specs=[VMEM, VMEM],
        out_specs=HBM,
        scratch_shapes=[
            pltpu.VMEM((messages, cells), f32),
            pltpu.VMEM((params, tiles, cells), f32),
            pltpu.SemaphoreType.DMA((params,)),
        ],
        compiler_params=pltpu.CompilerParams(vmem_limit_bytes=16 * MIB),
        name="add",
    )(requests, returned)
    return residual, gradient[None]


def solution(mesh):
    return jax.shard_map(
        per_device,
        mesh=mesh,
        in_specs=(
            P(AXES, None, None),
            P(AXES, None),
            P(AXES, None),
            P(AXES, None),
            P(AXES),
            P(AXES),
            P(AXES, None, None, None),
        ),
        out_specs=(P(AXES, None), P(AXES, None, None, None)),
        check_vma=False,
    )
```

```python
import functools

import jax
import jax.numpy as jnp
from jax import lax
from jax.experimental import pallas as pl
from jax.experimental.pallas import tpu as pltpu
from jax.sharding import PartitionSpec as P

SLOTS = 3
MIB = 1 << 20
AXES = ("zx", "core", "dep")
GROUP = ("zx", "dep")
ORDER = ("core", "zx", "dep")
VMEM = pl.BlockSpec(memory_space=pltpu.VMEM)
SMEM = pl.BlockSpec(memory_space=pltpu.SMEM)
HBM = pl.BlockSpec(memory_space=pltpu.HBM)


def in_hbm(array):
    return pltpu.with_memory_space_constraint(array, pltpu.HBM)


def iota(shape, axis):
    return lax.broadcasted_iota(jnp.int32, shape, axis)


def column_of(row):
    wide = jnp.broadcast_to(row.astype(jnp.float32), (128, row.shape[1]))
    return wide.T


def plan_kernel(
    count_ref, brick_hbm, tile_hbm, model_hbm, wanted_ref, near_ref, far_ref, low_ref, brick_ref, tile_ref, model_ref, sems,
    *, per_ray, members, depth,
):
    brick_copy = pltpu.make_async_copy(brick_hbm, brick_ref, sems.at[0])
    tile_copy = pltpu.make_async_copy(tile_hbm, tile_ref, sems.at[1])
    brick_copy.start()
    tile_copy.start()
    params, _, cells = model_ref.shape
    for p in range(params):
        pltpu.make_async_copy(model_hbm.at[p], model_ref.at[p], sems.at[2 + p]).start()
    hits = brick_ref.shape[1]
    live = count_ref[0] * per_ray
    brick_copy.wait()
    tile_copy.wait()
    named = brick_ref[...]
    brick = named.astype(jnp.float32)
    down = column_of(brick)
    ranks = []
    for start in range(0, hits, 128):
        across = brick[:, start : start + 128]
        first = iota((hits, 128), 0)
        earlier = (down == across) & (first < iota((hits, 128), 1) + start) & (first < live)
        ranks.append(jnp.sum(earlier.astype(jnp.float32), axis=0, keepdims=True))
    rank = jnp.concatenate(ranks, axis=1)
    core = lax.rem(lax.div(named, depth), 2)
    member = lax.div(named, 2 * depth) * depth + lax.rem(named, depth)
    core, member = core.astype(jnp.float32), member.astype(jnp.float32)
    alive = iota((1, hits), 1) < live
    near = jnp.where(alive, (core * SLOTS + rank) * members + member, -1.0)
    near_ref[...] = near
    far_ref[...] = jnp.where(alive, (rank * 2 + core) * members + member, -1.0)
    tile = tile_ref[...].astype(jnp.float32) + 1.0
    owner = iota((members, 1), 0).astype(jnp.float32)
    lane = iota((members, 128), 1)
    wanted = jnp.zeros((members, 128), jnp.float32)
    for k in range(2 * SLOTS):
        hit = jnp.where(near == owner + float(k * members), tile, 0.0)
        wanted = jnp.where(lane == k, jnp.sum(hit, axis=1, keepdims=True), wanted)
    wanted_ref[...] = wanted.astype(jnp.int32)
    for p in range(params):
        pltpu.make_async_copy(model_hbm.at[p], model_ref.at[p], sems.at[2 + p]).wait()
        low_ref[:, p * cells : (p + 1) * cells] = model_ref[p].astype(jnp.bfloat16)


def spread(product, spread_ref, first, slots, rows, params, cells):
    for k in range(product.shape[0] // rows):
        for p in range(params):
            part = product[k * rows : (k + 1) * rows, p * cells : (p + 1) * cells]
            spread_ref[pl.ds((first + k) * params + p, rows, stride=slots * params), :] = part


def gathered(spread_ref, slots, rows, params):
    blocks = []
    for k in range(slots):
        parts = [spread_ref[pl.ds(k * params + p, rows, stride=slots * params), :] for p in range(params)]
        blocks.append(jnp.concatenate(parts, axis=1).astype(jnp.bfloat16))
    return jnp.concatenate(blocks, axis=0)


def fetch_kernel(wanted_ref, own_ref, other_ref, out_ref, spread_ref, *, params):
    tiles = own_ref.shape[0]
    cells = own_ref.shape[1] // params
    members = wanted_ref.shape[0]
    even = lax.axis_index("core") == 0
    own, other = own_ref[...], other_ref[...]
    wanted = wanted_ref[...]
    for core in range(2):
        model = jnp.where(even, own, other) if core == 0 else jnp.where(even, other, own)
        picks = []
        for k in range(core * SLOTS, (core + 1) * SLOTS):
            pick = wanted[:, k : k + 1] == iota((members, tiles), 1) + 1
            picks.append(pick.astype(jnp.float32).astype(jnp.bfloat16))
        product = jnp.dot(jnp.concatenate(picks, axis=0), model, preferred_element_type=jnp.float32)
        spread(product, spread_ref, core * SLOTS, 2 * SLOTS, members, params, cells)
    out_ref[...] = spread_ref[...].astype(jnp.bfloat16)


def rays_kernel(
    count_ref, near_ref, far_ref, early_ref, arrived_ref, coefficient_hbm, observed_hbm, kernel_ref,
    residual_ref, out_ref, coefficient_ref, observed_ref, spread_ref, own_ref, grad_ref, total_ref, twice_ref,
    held_ref, sems, small_sems,
    *, per_ray, params, group,
):
    del early_ref
    hits, bands, cells = held_ref.shape
    rays = observed_ref.shape[0]
    devices = arrived_ref.shape[0] // (SLOTS * params)
    chunks = rays // group
    step = group * per_ray

    def fetch(i):
        part = pl.ds(i * step, step)
        return pltpu.make_async_copy(kernel_ref.at[part], held_ref.at[part], sems.at[i])

    coefficient_copy = pltpu.make_async_copy(coefficient_hbm, coefficient_ref, small_sems.at[0])
    observed_copy = pltpu.make_async_copy(observed_hbm, observed_ref, small_sems.at[1])
    coefficient_copy.start()
    for i in range(chunks):
        fetch(i).start()
    observed_copy.start()
    spread_ref[...] = arrived_ref[...].astype(jnp.float32)
    slot_down = column_of(near_ref[...])
    picks = []
    for start in range(0, SLOTS * devices, 128):
        pick = slot_down == (iota((hits, 128), 1) + start).astype(jnp.float32)
        picks.append(pick.astype(jnp.float32).astype(jnp.bfloat16))
    pick = jnp.concatenate(picks, axis=1)
    blocks = gathered(spread_ref, 2 * SLOTS, devices // 2, params)
    for p in range(0, params, 2):
        own = jnp.dot(pick, blocks[:, p * cells : (p + 2) * cells], preferred_element_type=jnp.float32)
        for q in range(2):
            part = own[:, q * cells : (q + 1) * cells].reshape(rays, per_ray, cells)
            own_ref[:, (p + q) * per_ray : (p + q + 1) * per_ray, :] = part

    lane = iota((per_ray, 128), 1)
    low = lane < bands
    pairs = per_ray * bands // 128
    mine = [iota((per_ray, 128), 0) == 2 * j + lane // bands for j in range(pairs)]

    def scales(rows):
        scale = []
        for half in range(params // 2):
            two = coefficient_ref[rows, half * 128 : half * 128 + 128]
            turned = pltpu.roll(two, bands, 1)
            scale.append(jnp.where(low, two, turned))
            scale.append(jnp.where(low, turned, two))
        return scale

    def rows_of(ray):
        return pl.ds(pl.multiple_of(ray * per_ray, per_ray), per_ray)

    def sense(ray):
        rows = rows_of(ray)
        sheet = held_ref[rows].reshape(per_ray * bands, cells)
        sensed = lax.dot_general(
            own_ref[ray].astype(jnp.bfloat16), sheet, (((1,), (1,)), ((), ())), preferred_element_type=jnp.float32
        )
        scale = scales(rows)
        total = jnp.zeros((per_ray, 128), jnp.float32)
        for j in range(pairs):
            part = scale[0] * sensed[:per_ray, j * 128 : (j + 1) * 128]
            for p in range(1, params):
                part += scale[p] * sensed[p * per_ray : (p + 1) * per_ray, j * 128 : (j + 1) * 128]
            total = jnp.where(mine[j], part, total)
        total_ref[rows, :] = total

    coefficient_copy.wait()

    def forward(g, carry):
        fetch(g).wait()
        for n in range(group):
            sense(g * group + n)
        return carry

    lax.fori_loop(0, chunks, forward, 0)

    predicted = total_ref[pl.ds(0, rays, stride=per_ray), :]
    for i in range(1, per_ray):
        predicted += total_ref[pl.ds(i, rays, stride=per_ray), :]
    predicted = predicted + pltpu.roll(predicted, bands, 1)
    observed_copy.wait()
    seen = observed_ref[...]
    seen = jnp.concatenate([seen, seen], axis=1)
    residual = jnp.where(iota((rays, 128), 0) < count_ref[0], predicted - seen, 0.0)
    residual_ref[...] = residual[:, :bands]
    twice_ref[...] = residual

    rows_all = params * per_ray
    keep = [
        (iota((rows_all, 128), 0) % per_ray == 2 * j + iota((rows_all, 128), 1) // bands)
        .astype(jnp.float32)
        .astype(jnp.bfloat16)
        for j in range(pairs)
    ]

    def adjoint(ray):
        rows = rows_of(ray)
        sheet = held_ref[rows].reshape(per_ray * bands, cells)
        residual = twice_ref[pl.ds(ray, 1), :]
        weight = jnp.concatenate([p * residual for p in scales(rows)], axis=0).astype(jnp.bfloat16)
        weight = jnp.concatenate([weight * keep[j] for j in range(pairs)], axis=1)
        grad_ref[ray] = jnp.dot(weight, sheet, preferred_element_type=jnp.float32)

    for n in range(rays):
        adjoint(n)

    grad = jnp.concatenate(
        [grad_ref[:, p * per_ray : (p + 1) * per_ray, :].reshape(hits, cells) for p in range(params)], axis=1
    ).astype(jnp.bfloat16)
    place = far_ref[...] == iota((SLOTS * devices, hits), 0).astype(jnp.float32)
    place = place.astype(jnp.float32).astype(jnp.bfloat16)
    product = jnp.dot(place, grad, preferred_element_type=jnp.float32)
    spread(product, spread_ref, 0, SLOTS, devices, params, cells)
    out_ref[...] = spread_ref[...].astype(jnp.bfloat16)


def sum_kernel(mine_ref, other_ref, returned_ref, out_hbm, spread_ref, out_ref, sems):
    params, tiles, cells = out_ref.shape
    members = mine_ref.shape[0]
    spread_ref[...] = returned_ref[...].astype(jnp.float32)
    even = lax.axis_index("core") == 0
    mine = mine_ref[...].astype(jnp.float32)
    other = other_ref[...].astype(jnp.float32)
    asked = [jnp.where(even, mine, other).T, jnp.where(even, other, mine).T]
    picks = []
    for k in range(SLOTS):
        for rows in asked:
            row = jnp.where(even, rows[k : k + 1], rows[SLOTS + k : SLOTS + k + 1])
            pick = row == (iota((tiles, members), 0) + 1).astype(jnp.float32)
            picks.append(pick.astype(jnp.float32).astype(jnp.bfloat16))
    pick = jnp.concatenate(picks, axis=1)
    blocks = gathered(spread_ref, SLOTS, 2 * members, params)
    for p in range(0, params, 2):
        total = jnp.dot(pick, blocks[:, p * cells : (p + 2) * cells], preferred_element_type=jnp.float32)
        for q in range(2):
            out_ref[p + q] = total[:, q * cells : (q + 1) * cells]
            pltpu.make_async_copy(out_ref.at[p + q], out_hbm.at[p + q], sems.at[p + q]).start()
    for p in range(params):
        pltpu.make_async_copy(out_ref.at[p], out_hbm.at[p], sems.at[p]).wait()


def exchange(rows, axes, devices, params, cells):
    slots = rows.shape[0] // (devices * params)
    sent = rows.reshape(devices, slots, params, cells)
    back = lax.all_to_all(sent, axes, split_axis=0, concat_axis=0, tiled=True)
    return back.reshape(devices * slots * params, cells)


def per_device(kernel, coefficient, observed, ray_brick, tile_index, ray_count, earth_model):
    hits, bands, cells = kernel.shape
    params, tiles = earth_model.shape[1:3]
    rays = observed.shape[0]
    per_ray = hits // rays
    depth = lax.axis_size("dep")
    members = lax.axis_size("zx") * depth
    devices = 2 * members
    swap = [(0, 1), (1, 0)]
    messages = devices * SLOTS * params
    f32, bf16 = jnp.float32, jnp.bfloat16
    shape = jax.ShapeDtypeStruct

    wanted, near, far, model = pl.pallas_call(
        functools.partial(plan_kernel, per_ray=per_ray, members=members, depth=depth),
        out_shape=(
            shape((members, 128), jnp.int32),
            shape((1, hits), f32),
            shape((1, hits), f32),
            shape((tiles, params * cells), bf16),
        ),
        in_specs=[SMEM, HBM, HBM, HBM],
        out_specs=(VMEM, VMEM, VMEM, VMEM),
        scratch_shapes=[
            pltpu.VMEM((1, hits), jnp.int32),
            pltpu.VMEM((1, hits), jnp.int32),
            pltpu.VMEM((params, tiles, cells), f32),
            pltpu.SemaphoreType.DMA((2 + params,)),
        ],
        compiler_params=pltpu.CompilerParams(vmem_limit_bytes=8 * MIB),
        name="plan",
    )(ray_count, in_hbm(ray_brick.reshape(1, hits)), in_hbm(tile_index.reshape(1, hits)), in_hbm(earth_model[0]))
    other_model = lax.ppermute(model, "core", swap)
    requests = lax.all_to_all(wanted.reshape(members, 1, 128), GROUP, split_axis=0, concat_axis=0, tiled=True)
    requests = requests.reshape(members, 128)
    other_requests = lax.ppermute(requests, "core", swap)
    blocks = pl.pallas_call(
        functools.partial(fetch_kernel, params=params),
        out_shape=shape((messages, cells), bf16),
        in_specs=[VMEM, VMEM, VMEM],
        out_specs=VMEM,
        scratch_shapes=[pltpu.VMEM((messages, cells), f32)],
        compiler_params=pltpu.CompilerParams(vmem_limit_bytes=16 * MIB),
        name="fetch",
    )(requests, model, other_model)
    arrived = exchange(blocks, GROUP, members, params, cells)
    group = 16
    residual, outgoing = pl.pallas_call(
        functools.partial(rays_kernel, per_ray=per_ray, params=params, group=group),
        out_shape=(shape((rays, bands), f32), shape((messages, cells), bf16)),
        in_specs=[SMEM, VMEM, VMEM, VMEM, VMEM, HBM, HBM, HBM],
        out_specs=(VMEM, VMEM),
        scratch_shapes=[
            pltpu.VMEM((hits, params * bands), f32),
            pltpu.VMEM((rays, bands), f32),
            pltpu.VMEM((messages, cells), f32),
            pltpu.VMEM((rays, params * per_ray, cells), f32),
            pltpu.VMEM((rays, params * per_ray, cells), f32),
            pltpu.VMEM((hits, 128), f32),
            pltpu.VMEM((rays, 128), f32),
            pltpu.VMEM((hits, bands, cells), bf16),
            pltpu.SemaphoreType.DMA((rays // group,)),
            pltpu.SemaphoreType.DMA((2,)),
        ],
        compiler_params=pltpu.CompilerParams(vmem_limit_bytes=28 * MIB),
        name="rays",
    )(ray_count, near, far, other_requests, arrived, in_hbm(coefficient), in_hbm(observed), in_hbm(kernel))
    returned = exchange(outgoing, ORDER, devices, params, cells)
    gradient = pl.pallas_call(
        sum_kernel,
        out_shape=shape((params, tiles, cells), f32),
        in_specs=[VMEM, VMEM, VMEM],
        out_specs=HBM,
        scratch_shapes=[
            pltpu.VMEM((messages, cells), f32),
            pltpu.VMEM((params, tiles, cells), f32),
            pltpu.SemaphoreType.DMA((params,)),
        ],
        compiler_params=pltpu.CompilerParams(vmem_limit_bytes=16 * MIB),
        name="add",
    )(requests, other_requests, returned)
    return residual, gradient[None]


def solution(mesh):
    lat, dep = mesh.devices.shape
    chips = jax.sharding.Mesh(mesh.devices.reshape(lat // 2, 2, dep), AXES)
    return jax.shard_map(
        per_device,
        mesh=chips,
        in_specs=(
            P(AXES, None, None),
            P(AXES, None),
            P(AXES, None),
            P(AXES, None),
            P(AXES),
            P(AXES),
            P(AXES, None, None, None),
        ),
        out_specs=(P(AXES, None), P(AXES, None, None, None)),
        check_vma=False,
    )
```

```python
import functools

import jax
import jax.numpy as jnp
from jax import lax
from jax.experimental import pallas as pl
from jax.experimental.pallas import tpu as pltpu
from jax.sharding import PartitionSpec as P

SLOTS = 3
MIB = 1 << 20
AXES = ("lat", "dep")
VMEM = pl.BlockSpec(memory_space=pltpu.VMEM)
SMEM = pl.BlockSpec(memory_space=pltpu.SMEM)
HBM = pl.BlockSpec(memory_space=pltpu.HBM)


def in_hbm(array):
    return pltpu.with_memory_space_constraint(array, pltpu.HBM)


def iota(shape, axis):
    return lax.broadcasted_iota(jnp.int32, shape, axis)


def column_of(row):
    wide = jnp.broadcast_to(row.astype(jnp.float32), (128, row.shape[1]))
    return wide.T


def plan_kernel(
    count_ref, brick_hbm, tile_hbm, model_hbm, wanted_ref, slot_ref, low_ref, brick_ref, tile_ref, model_ref, sems,
    *, per_ray, devices,
):
    brick_copy = pltpu.make_async_copy(brick_hbm, brick_ref, sems.at[0])
    tile_copy = pltpu.make_async_copy(tile_hbm, tile_ref, sems.at[1])
    brick_copy.start()
    tile_copy.start()
    params, _, cells = model_ref.shape
    for p in range(params):
        pltpu.make_async_copy(model_hbm.at[p], model_ref.at[p], sems.at[2 + p]).start()
    hits = brick_ref.shape[1]
    live = count_ref[0] * per_ray
    brick_copy.wait()
    tile_copy.wait()
    brick = brick_ref[...].astype(jnp.float32)
    down = column_of(brick)
    ranks = []
    for start in range(0, hits, 128):
        across = brick[:, start : start + 128]
        first = iota((hits, 128), 0)
        earlier = (down == across) & (first < iota((hits, 128), 1) + start) & (first < live)
        ranks.append(jnp.sum(earlier.astype(jnp.float32), axis=0, keepdims=True))
    rank = jnp.concatenate(ranks, axis=1)
    alive = iota((1, hits), 1) < live
    slot = jnp.where(alive, rank * devices + brick, -1.0)
    slot_ref[...] = slot
    tile = tile_ref[...].astype(jnp.float32) + 1.0
    owner = iota((devices, 1), 0).astype(jnp.float32)
    lane = iota((devices, 128), 1)
    wanted = jnp.zeros((devices, 128), jnp.float32)
    for k in range(SLOTS):
        hit = jnp.where(slot == owner + float(k * devices), tile, 0.0)
        wanted = jnp.where(lane == k, jnp.sum(hit, axis=1, keepdims=True), wanted)
    wanted_ref[...] = wanted.astype(jnp.int32)
    for p in range(params):
        pltpu.make_async_copy(model_hbm.at[p], model_ref.at[p], sems.at[2 + p]).wait()
        low_ref[:, p * cells : (p + 1) * cells] = model_ref[p].astype(jnp.bfloat16)


def spread(product, spread_ref, rows, params, cells):
    for k in range(SLOTS):
        for p in range(params):
            part = product[k * rows : (k + 1) * rows, p * cells : (p + 1) * cells]
            spread_ref[pl.ds(k * params + p, rows, stride=SLOTS * params), :] = part


def gathered(spread_ref, k, rows, params):
    parts = [spread_ref[pl.ds(k * params + p, rows, stride=SLOTS * params), :] for p in range(params)]
    return jnp.concatenate(parts, axis=1).astype(jnp.bfloat16)


def fetch_kernel(wanted_ref, model_ref, out_ref, spread_ref, *, params):
    tiles = model_ref.shape[0]
    cells = model_ref.shape[1] // params
    devices = wanted_ref.shape[0]
    model = model_ref[...]
    wanted = wanted_ref[...]
    picks = []
    for k in range(SLOTS):
        pick = wanted[:, k : k + 1] == iota((devices, tiles), 1) + 1
        picks.append(pick.astype(jnp.float32).astype(jnp.bfloat16))
    pick = jnp.concatenate(picks, axis=0)
    spread(jnp.dot(pick, model, preferred_element_type=jnp.float32), spread_ref, devices, params, cells)
    out_ref[...] = spread_ref[...].astype(jnp.bfloat16)


def rays_kernel(
    count_ref, slot_ref, arrived_ref, coefficient_hbm, observed_hbm, kernel_ref,
    residual_ref, out_ref, coefficient_ref, observed_ref, spread_ref, own_ref, grad_ref, total_ref, twice_ref,
    held_ref, sems, small_sems,
    *, per_ray, params, group,
):
    hits, bands, cells = held_ref.shape
    rays = observed_ref.shape[0]
    devices = arrived_ref.shape[0] // (SLOTS * params)
    chunks = rays // group
    step = group * per_ray

    def fetch(i):
        part = pl.ds(i * step, step)
        return pltpu.make_async_copy(kernel_ref.at[part], held_ref.at[part], sems.at[i])

    coefficient_copy = pltpu.make_async_copy(coefficient_hbm, coefficient_ref, small_sems.at[0])
    observed_copy = pltpu.make_async_copy(observed_hbm, observed_ref, small_sems.at[1])
    coefficient_copy.start()
    for i in range(chunks):
        fetch(i).start()
    observed_copy.start()
    spread_ref[...] = arrived_ref[...].astype(jnp.float32)
    slot = slot_ref[...]
    slot_down = column_of(slot)
    picks = []
    for start in range(0, SLOTS * devices, 128):
        pick = slot_down == (iota((hits, 128), 1) + start).astype(jnp.float32)
        picks.append(pick.astype(jnp.float32).astype(jnp.bfloat16))
    pick = jnp.concatenate(picks, axis=1)
    blocks = jnp.concatenate([gathered(spread_ref, k, devices, params) for k in range(SLOTS)], axis=0)
    for p in range(0, params, 2):
        own = jnp.dot(pick, blocks[:, p * cells : (p + 2) * cells], preferred_element_type=jnp.float32)
        for q in range(2):
            part = own[:, q * cells : (q + 1) * cells].reshape(rays, per_ray, cells)
            own_ref[:, (p + q) * per_ray : (p + q + 1) * per_ray, :] = part

    lane = iota((per_ray, 128), 1)
    low = lane < bands
    pairs = per_ray * bands // 128
    mine = [iota((per_ray, 128), 0) == 2 * j + lane // bands for j in range(pairs)]

    def scales(rows):
        scale = []
        for half in range(params // 2):
            two = coefficient_ref[rows, half * 128 : half * 128 + 128]
            turned = pltpu.roll(two, bands, 1)
            scale.append(jnp.where(low, two, turned))
            scale.append(jnp.where(low, turned, two))
        return scale

    def rows_of(ray):
        return pl.ds(pl.multiple_of(ray * per_ray, per_ray), per_ray)

    blank = jnp.zeros((params * per_ray, cells), jnp.bfloat16)

    def sense(first):
        rows = pl.ds(pl.multiple_of(first * per_ray, 2 * per_ray), 2 * per_ray)
        sheet = held_ref[rows].reshape(2, per_ray * bands, cells)
        sheet = jnp.concatenate([sheet[0], sheet[1]], axis=1)
        block = own_ref[pl.ds(first, 2)].astype(jnp.bfloat16)
        block = jnp.concatenate(
            [jnp.concatenate([block[0], blank], axis=1), jnp.concatenate([blank, block[1]], axis=1)], axis=0
        )
        both = lax.dot_general(block, sheet, (((1,), (1,)), ((), ())), preferred_element_type=jnp.float32)
        for n in range(2):
            sensed = both[n * params * per_ray : (n + 1) * params * per_ray]
            rows = rows_of(first + n)
            scale = scales(rows)
            total = jnp.zeros((per_ray, 128), jnp.float32)
            for j in range(pairs):
                part = scale[0] * sensed[:per_ray, j * 128 : (j + 1) * 128]
                for p in range(1, params):
                    part += scale[p] * sensed[p * per_ray : (p + 1) * per_ray, j * 128 : (j + 1) * 128]
                total = jnp.where(mine[j], part, total)
            total_ref[rows, :] = total

    coefficient_copy.wait()

    def forward(g, carry):
        fetch(g).wait()
        for n in range(0, group, 2):
            sense(g * group + n)
        return carry

    lax.fori_loop(0, chunks, forward, 0)

    predicted = total_ref[pl.ds(0, rays, stride=per_ray), :]
    for i in range(1, per_ray):
        predicted += total_ref[pl.ds(i, rays, stride=per_ray), :]
    predicted = predicted + pltpu.roll(predicted, bands, 1)
    observed_copy.wait()
    seen = observed_ref[...]
    seen = jnp.concatenate([seen, seen], axis=1)
    residual = jnp.where(iota((rays, 128), 0) < count_ref[0], predicted - seen, 0.0)
    residual_ref[...] = residual[:, :bands]
    twice_ref[...] = residual

    rows_all = params * per_ray
    keep = [
        (iota((rows_all, 128), 0) % per_ray == 2 * j + iota((rows_all, 128), 1) // bands)
        .astype(jnp.float32)
        .astype(jnp.bfloat16)
        for j in range(pairs)
    ]

    def adjoint(ray):
        rows = rows_of(ray)
        sheet = held_ref[rows].reshape(per_ray * bands, cells)
        residual = twice_ref[pl.ds(ray, 1), :]
        weight = jnp.concatenate([p * residual for p in scales(rows)], axis=0).astype(jnp.bfloat16)
        weight = jnp.concatenate([weight * keep[j] for j in range(pairs)], axis=1)
        grad_ref[ray] = jnp.dot(weight, sheet, preferred_element_type=jnp.float32)

    for n in range(rays):
        adjoint(n)

    grad = jnp.concatenate(
        [grad_ref[:, p * per_ray : (p + 1) * per_ray, :].reshape(hits, cells) for p in range(params)], axis=1
    ).astype(jnp.bfloat16)
    place = slot == iota((SLOTS * devices, hits), 0).astype(jnp.float32)
    place = place.astype(jnp.float32).astype(jnp.bfloat16)
    spread(jnp.dot(place, grad, preferred_element_type=jnp.float32), spread_ref, devices, params, cells)
    out_ref[...] = spread_ref[...].astype(jnp.bfloat16)


def sum_kernel(wanted_ref, returned_ref, out_hbm, spread_ref, out_ref, sems):
    params, tiles, cells = out_ref.shape
    devices = wanted_ref.shape[0]
    spread_ref[...] = returned_ref[...].astype(jnp.float32)
    across = wanted_ref[...].astype(jnp.float32).T
    picks = []
    for k in range(SLOTS):
        pick = across[k : k + 1, :] == (iota((tiles, devices), 0) + 1).astype(jnp.float32)
        picks.append(pick.astype(jnp.float32).astype(jnp.bfloat16))
    pick = jnp.concatenate(picks, axis=1)
    blocks = jnp.concatenate([gathered(spread_ref, k, devices, params) for k in range(SLOTS)], axis=0)
    for p in range(0, params, 2):
        total = jnp.dot(pick, blocks[:, p * cells : (p + 2) * cells], preferred_element_type=jnp.float32)
        for q in range(2):
            out_ref[p + q] = total[:, q * cells : (q + 1) * cells]
            pltpu.make_async_copy(out_ref.at[p + q], out_hbm.at[p + q], sems.at[p + q]).start()
    for p in range(params):
        pltpu.make_async_copy(out_ref.at[p], out_hbm.at[p], sems.at[p]).wait()


def exchange(rows, devices, params, cells):
    sent = rows.reshape(devices, SLOTS, params, cells)
    back = lax.all_to_all(sent, AXES, split_axis=0, concat_axis=0, tiled=True)
    return back.reshape(devices * SLOTS * params, cells)


def per_device(kernel, coefficient, observed, ray_brick, tile_index, ray_count, earth_model):
    hits, bands, cells = kernel.shape
    params, tiles = earth_model.shape[1:3]
    rays = observed.shape[0]
    per_ray = hits // rays
    devices = lax.axis_size("lat") * lax.axis_size("dep")
    messages = devices * SLOTS * params
    f32, bf16 = jnp.float32, jnp.bfloat16
    shape = jax.ShapeDtypeStruct

    wanted, slot, model = pl.pallas_call(
        functools.partial(plan_kernel, per_ray=per_ray, devices=devices),
        out_shape=(
            shape((devices, 128), jnp.int32),
            shape((1, hits), f32),
            shape((tiles, params * cells), bf16),
        ),
        in_specs=[SMEM, HBM, HBM, HBM],
        out_specs=(VMEM, VMEM, VMEM),
        scratch_shapes=[
            pltpu.VMEM((1, hits), jnp.int32),
            pltpu.VMEM((1, hits), jnp.int32),
            pltpu.VMEM((params, tiles, cells), f32),
            pltpu.SemaphoreType.DMA((2 + params,)),
        ],
        compiler_params=pltpu.CompilerParams(vmem_limit_bytes=8 * MIB),
        name="plan",
    )(ray_count, in_hbm(ray_brick.reshape(1, hits)), in_hbm(tile_index.reshape(1, hits)), in_hbm(earth_model[0]))
    requests = lax.all_to_all(wanted.reshape(devices, 1, 128), AXES, split_axis=0, concat_axis=0, tiled=True)
    requests = requests.reshape(devices, 128)
    blocks = pl.pallas_call(
        functools.partial(fetch_kernel, params=params),
        out_shape=shape((messages, cells), bf16),
        in_specs=[VMEM, VMEM],
        out_specs=VMEM,
        scratch_shapes=[pltpu.VMEM((messages, cells), f32)],
        compiler_params=pltpu.CompilerParams(vmem_limit_bytes=16 * MIB),
        name="fetch",
    )(requests, model)
    arrived = exchange(blocks, devices, params, cells)
    group = 16
    residual, outgoing = pl.pallas_call(
        functools.partial(rays_kernel, per_ray=per_ray, params=params, group=group),
        out_shape=(shape((rays, bands), f32), shape((messages, cells), bf16)),
        in_specs=[SMEM, VMEM, VMEM, HBM, HBM, HBM],
        out_specs=(VMEM, VMEM),
        scratch_shapes=[
            pltpu.VMEM((hits, params * bands), f32),
            pltpu.VMEM((rays, bands), f32),
            pltpu.VMEM((messages, cells), f32),
            pltpu.VMEM((rays, params * per_ray, cells), f32),
            pltpu.VMEM((rays, params * per_ray, cells), f32),
            pltpu.VMEM((hits, 128), f32),
            pltpu.VMEM((rays, 128), f32),
            pltpu.VMEM((hits, bands, cells), bf16),
            pltpu.SemaphoreType.DMA((rays // group,)),
            pltpu.SemaphoreType.DMA((2,)),
        ],
        compiler_params=pltpu.CompilerParams(vmem_limit_bytes=28 * MIB),
        name="rays",
    )(ray_count, slot, arrived, in_hbm(coefficient), in_hbm(observed), in_hbm(kernel))
    returned = exchange(outgoing, devices, params, cells)
    gradient = pl.pallas_call(
        sum_kernel,
        out_shape=shape((params, tiles, cells), f32),
        in_specs=[VMEM, VMEM],
        out_specs=HBM,
        scratch_shapes=[
            pltpu.VMEM((messages, cells), f32),
            pltpu.VMEM((params, tiles, cells), f32),
            pltpu.SemaphoreType.DMA((params,)),
        ],
        compiler_params=pltpu.CompilerParams(vmem_limit_bytes=16 * MIB),
        name="add",
    )(requests, returned)
    return residual, gradient[None]


def solution(mesh):
    return jax.shard_map(
        per_device,
        mesh=mesh,
        in_specs=(
            P(AXES, None, None),
            P(AXES, None),
            P(AXES, None),
            P(AXES, None),
            P(AXES),
            P(AXES),
            P(AXES, None, None, None),
        ),
        out_specs=(P(AXES, None), P(AXES, None, None, None)),
        check_vma=False,
    )
```

```python
import functools

import jax
import jax.numpy as jnp
from jax import lax
from jax.experimental import pallas as pl
from jax.experimental.pallas import tpu as pltpu
from jax.sharding import PartitionSpec as P

SLOTS = 3
MIB = 1 << 20
AXES = ("lat", "dep")
VMEM = pl.BlockSpec(memory_space=pltpu.VMEM)
SMEM = pl.BlockSpec(memory_space=pltpu.SMEM)
HBM = pl.BlockSpec(memory_space=pltpu.HBM)


def in_hbm(array):
    return pltpu.with_memory_space_constraint(array, pltpu.HBM)


def iota(shape, axis):
    return lax.broadcasted_iota(jnp.int32, shape, axis)


def column_of(row):
    wide = jnp.broadcast_to(row.astype(jnp.float32), (128, row.shape[1]))
    return wide.T


def plan_kernel(
    count_ref, brick_hbm, tile_hbm, model_hbm, wanted_ref, slot_ref, low_ref, brick_ref, tile_ref, model_ref, sems,
    *, per_ray, devices,
):
    brick_copy = pltpu.make_async_copy(brick_hbm, brick_ref, sems.at[0])
    tile_copy = pltpu.make_async_copy(tile_hbm, tile_ref, sems.at[1])
    brick_copy.start()
    tile_copy.start()
    params, _, cells = model_ref.shape
    for p in range(params):
        pltpu.make_async_copy(model_hbm.at[p], model_ref.at[p], sems.at[2 + p]).start()
    hits = brick_ref.shape[1]
    live = count_ref[0] * per_ray
    brick_copy.wait()
    tile_copy.wait()
    brick = brick_ref[...].astype(jnp.float32)
    down = column_of(brick)
    ranks = []
    for start in range(0, hits, 128):
        across = brick[:, start : start + 128]
        first = iota((hits, 128), 0)
        earlier = (down == across) & (first < iota((hits, 128), 1) + start) & (first < live)
        ranks.append(jnp.sum(earlier.astype(jnp.float32), axis=0, keepdims=True))
    rank = jnp.concatenate(ranks, axis=1)
    alive = iota((1, hits), 1) < live
    slot = jnp.where(alive, rank * devices + brick, -1.0)
    slot_ref[...] = slot
    tile = tile_ref[...].astype(jnp.float32) + 1.0
    owner = iota((devices, 1), 0).astype(jnp.float32)
    lane = iota((devices, 128), 1)
    wanted = jnp.zeros((devices, 128), jnp.float32)
    for k in range(SLOTS):
        hit = jnp.where(slot == owner + float(k * devices), tile, 0.0)
        wanted = jnp.where(lane == k, jnp.sum(hit, axis=1, keepdims=True), wanted)
    wanted_ref[...] = wanted.astype(jnp.int32)
    for p in range(params):
        pltpu.make_async_copy(model_hbm.at[p], model_ref.at[p], sems.at[2 + p]).wait()
        low_ref[:, p * cells : (p + 1) * cells] = model_ref[p].astype(jnp.bfloat16)


def spread(product, spread_ref, rows, params, cells):
    for k in range(SLOTS):
        for p in range(params):
            part = product[k * rows : (k + 1) * rows, p * cells : (p + 1) * cells]
            spread_ref[pl.ds(k * params + p, rows, stride=SLOTS * params), :] = part


def gathered(spread_ref, k, rows, params):
    parts = [spread_ref[pl.ds(k * params + p, rows, stride=SLOTS * params), :] for p in range(params)]
    return jnp.concatenate(parts, axis=1).astype(jnp.bfloat16)


def fetch_kernel(wanted_ref, model_ref, out_ref, spread_ref, *, params):
    tiles = model_ref.shape[0]
    cells = model_ref.shape[1] // params
    devices = wanted_ref.shape[0]
    model = model_ref[...]
    wanted = wanted_ref[...]
    picks = []
    for k in range(SLOTS):
        pick = wanted[:, k : k + 1] == iota((devices, tiles), 1) + 1
        picks.append(pick.astype(jnp.float32).astype(jnp.bfloat16))
    pick = jnp.concatenate(picks, axis=0)
    spread(jnp.dot(pick, model, preferred_element_type=jnp.float32), spread_ref, devices, params, cells)
    out_ref[...] = spread_ref[...].astype(jnp.bfloat16)


def rays_kernel(
    count_ref, slot_ref, arrived_ref, coefficient_hbm, observed_hbm, kernel_ref,
    residual_ref, out_ref, coefficient_ref, observed_ref, spread_ref, own_ref, grad_ref, total_ref, twice_ref,
    held_ref, sems, small_sems,
    *, per_ray, params, group,
):
    hits, bands, cells = held_ref.shape
    rays = observed_ref.shape[0]
    devices = arrived_ref.shape[0] // (SLOTS * params)
    chunks = rays // group
    step = group * per_ray

    def fetch(i):
        part = pl.ds(i * step, step)
        return pltpu.make_async_copy(kernel_ref.at[part], held_ref.at[part], sems.at[i])

    coefficient_copy = pltpu.make_async_copy(coefficient_hbm, coefficient_ref, small_sems.at[0])
    observed_copy = pltpu.make_async_copy(observed_hbm, observed_ref, small_sems.at[1])
    fetch(0).start()
    coefficient_copy.start()
    for i in range(1, chunks):
        fetch(i).start()
    observed_copy.start()
    spread_ref[...] = arrived_ref[...].astype(jnp.float32)
    slot = slot_ref[...]
    slot_down = column_of(slot)
    picks = []
    for start in range(0, SLOTS * devices, 128):
        pick = slot_down == (iota((hits, 128), 1) + start).astype(jnp.float32)
        picks.append(pick.astype(jnp.float32).astype(jnp.bfloat16))
    pick = jnp.concatenate(picks, axis=1)
    blocks = jnp.concatenate([gathered(spread_ref, k, devices, params) for k in range(SLOTS)], axis=0)
    for p in range(0, params, 2):
        own = jnp.dot(pick, blocks[:, p * cells : (p + 2) * cells], preferred_element_type=jnp.float32)
        for q in range(2):
            part = own[:, q * cells : (q + 1) * cells].reshape(rays, per_ray, cells)
            own_ref[:, (p + q) * per_ray : (p + q + 1) * per_ray, :] = part

    lane = iota((per_ray, 128), 1)
    low = lane < bands
    pairs = per_ray * bands // 128
    mine = [iota((per_ray, 128), 0) == 2 * j + lane // bands for j in range(pairs)]

    def scales(rows):
        scale = []
        for half in range(params // 2):
            two = coefficient_ref[rows, half * 128 : half * 128 + 128]
            turned = pltpu.roll(two, bands, 1)
            scale.append(jnp.where(low, two, turned))
            scale.append(jnp.where(low, turned, two))
        return scale

    def rows_of(ray):
        return pl.ds(pl.multiple_of(ray * per_ray, per_ray), per_ray)

    blank = jnp.zeros((params * per_ray, cells), jnp.bfloat16)

    def sense(first):
        rows = pl.ds(pl.multiple_of(first * per_ray, 2 * per_ray), 2 * per_ray)
        sheet = held_ref[rows].reshape(2, per_ray * bands, cells)
        sheet = jnp.concatenate([sheet[0], sheet[1]], axis=1)
        block = own_ref[pl.ds(first, 2)].astype(jnp.bfloat16)
        block = jnp.concatenate(
            [jnp.concatenate([block[0], blank], axis=1), jnp.concatenate([blank, block[1]], axis=1)], axis=0
        )
        both = lax.dot_general(block, sheet, (((1,), (1,)), ((), ())), preferred_element_type=jnp.float32)
        for n in range(2):
            sensed = both[n * params * per_ray : (n + 1) * params * per_ray]
            rows = rows_of(first + n)
            scale = scales(rows)
            total = jnp.zeros((per_ray, 128), jnp.float32)
            for j in range(pairs):
                part = scale[0] * sensed[:per_ray, j * 128 : (j + 1) * 128]
                for p in range(1, params):
                    part += scale[p] * sensed[p * per_ray : (p + 1) * per_ray, j * 128 : (j + 1) * 128]
                total = jnp.where(mine[j], part, total)
            total_ref[rows, :] = total

    coefficient_copy.wait()

    def forward(g, carry):
        fetch(g).wait()
        for n in range(0, group, 2):
            sense(g * group + n)
        return carry

    lax.fori_loop(0, chunks, forward, 0)

    predicted = total_ref[pl.ds(0, rays, stride=per_ray), :]
    for i in range(1, per_ray):
        predicted += total_ref[pl.ds(i, rays, stride=per_ray), :]
    predicted = predicted + pltpu.roll(predicted, bands, 1)
    observed_copy.wait()
    seen = observed_ref[...]
    seen = jnp.concatenate([seen, seen], axis=1)
    residual = jnp.where(iota((rays, 128), 0) < count_ref[0], predicted - seen, 0.0)
    residual_ref[...] = residual[:, :bands]
    twice_ref[...] = residual

    rows_all = params * per_ray
    keep = [
        (iota((rows_all, 128), 0) % per_ray == 2 * j + iota((rows_all, 128), 1) // bands)
        .astype(jnp.float32)
        .astype(jnp.bfloat16)
        for j in range(pairs)
    ]

    def adjoint(ray):
        rows = rows_of(ray)
        sheet = held_ref[rows].reshape(per_ray * bands, cells)
        residual = twice_ref[pl.ds(ray, 1), :]
        weight = jnp.concatenate([p * residual for p in scales(rows)], axis=0).astype(jnp.bfloat16)
        weight = jnp.concatenate([weight * keep[j] for j in range(pairs)], axis=1)
        grad_ref[ray] = jnp.dot(weight, sheet, preferred_element_type=jnp.float32)

    for n in range(rays):
        adjoint(n)

    grad = jnp.concatenate(
        [grad_ref[:, p * per_ray : (p + 1) * per_ray, :].reshape(hits, cells) for p in range(params)], axis=1
    ).astype(jnp.bfloat16)
    place = slot == iota((SLOTS * devices, hits), 0).astype(jnp.float32)
    place = place.astype(jnp.float32).astype(jnp.bfloat16)
    spread(jnp.dot(place, grad, preferred_element_type=jnp.float32), spread_ref, devices, params, cells)
    out_ref[...] = spread_ref[...].astype(jnp.bfloat16)


def sum_kernel(wanted_ref, returned_ref, out_hbm, spread_ref, out_ref, sems):
    params, tiles, cells = out_ref.shape
    devices = wanted_ref.shape[0]
    spread_ref[...] = returned_ref[...].astype(jnp.float32)
    across = wanted_ref[...].astype(jnp.float32).T
    picks = []
    for k in range(SLOTS):
        pick = across[k : k + 1, :] == (iota((tiles, devices), 0) + 1).astype(jnp.float32)
        picks.append(pick.astype(jnp.float32).astype(jnp.bfloat16))
    pick = jnp.concatenate(picks, axis=1)
    blocks = jnp.concatenate([gathered(spread_ref, k, devices, params) for k in range(SLOTS)], axis=0)
    for p in range(0, params, 2):
        total = jnp.dot(pick, blocks[:, p * cells : (p + 2) * cells], preferred_element_type=jnp.float32)
        for q in range(2):
            out_ref[p + q] = total[:, q * cells : (q + 1) * cells]
            pltpu.make_async_copy(out_ref.at[p + q], out_hbm.at[p + q], sems.at[p + q]).start()
    for p in range(params):
        pltpu.make_async_copy(out_ref.at[p], out_hbm.at[p], sems.at[p]).wait()


def exchange(rows, devices, params, cells):
    sent = rows.reshape(devices, SLOTS, params, cells)
    back = lax.all_to_all(sent, AXES, split_axis=0, concat_axis=0, tiled=True)
    return back.reshape(devices * SLOTS * params, cells)


def per_device(kernel, coefficient, observed, ray_brick, tile_index, ray_count, earth_model):
    hits, bands, cells = kernel.shape
    params, tiles = earth_model.shape[1:3]
    rays = observed.shape[0]
    per_ray = hits // rays
    devices = lax.axis_size("lat") * lax.axis_size("dep")
    messages = devices * SLOTS * params
    f32, bf16 = jnp.float32, jnp.bfloat16
    shape = jax.ShapeDtypeStruct

    wanted, slot, model = pl.pallas_call(
        functools.partial(plan_kernel, per_ray=per_ray, devices=devices),
        out_shape=(
            shape((devices, 128), jnp.int32),
            shape((1, hits), f32),
            shape((tiles, params * cells), bf16),
        ),
        in_specs=[SMEM, HBM, HBM, HBM],
        out_specs=(VMEM, VMEM, VMEM),
        scratch_shapes=[
            pltpu.VMEM((1, hits), jnp.int32),
            pltpu.VMEM((1, hits), jnp.int32),
            pltpu.VMEM((params, tiles, cells), f32),
            pltpu.SemaphoreType.DMA((2 + params,)),
        ],
        compiler_params=pltpu.CompilerParams(vmem_limit_bytes=8 * MIB),
        name="plan",
    )(ray_count, in_hbm(ray_brick.reshape(1, hits)), in_hbm(tile_index.reshape(1, hits)), in_hbm(earth_model[0]))
    requests = lax.all_to_all(wanted.reshape(devices, 1, 128), AXES, split_axis=0, concat_axis=0, tiled=True)
    requests = requests.reshape(devices, 128)
    blocks = pl.pallas_call(
        functools.partial(fetch_kernel, params=params),
        out_shape=shape((messages, cells), bf16),
        in_specs=[VMEM, VMEM],
        out_specs=VMEM,
        scratch_shapes=[pltpu.VMEM((messages, cells), f32)],
        compiler_params=pltpu.CompilerParams(vmem_limit_bytes=16 * MIB),
        name="fetch",
    )(requests, model)
    arrived = exchange(blocks, devices, params, cells)
    group = 16
    residual, outgoing = pl.pallas_call(
        functools.partial(rays_kernel, per_ray=per_ray, params=params, group=group),
        out_shape=(shape((rays, bands), f32), shape((messages, cells), bf16)),
        in_specs=[SMEM, VMEM, VMEM, HBM, HBM, HBM],
        out_specs=(VMEM, VMEM),
        scratch_shapes=[
            pltpu.VMEM((hits, params * bands), f32),
            pltpu.VMEM((rays, bands), f32),
            pltpu.VMEM((messages, cells), f32),
            pltpu.VMEM((rays, params * per_ray, cells), f32),
            pltpu.VMEM((rays, params * per_ray, cells), f32),
            pltpu.VMEM((hits, 128), f32),
            pltpu.VMEM((rays, 128), f32),
            pltpu.VMEM((hits, bands, cells), bf16),
            pltpu.SemaphoreType.DMA((rays // group,)),
            pltpu.SemaphoreType.DMA((2,)),
        ],
        compiler_params=pltpu.CompilerParams(vmem_limit_bytes=28 * MIB),
        name="rays",
    )(ray_count, slot, arrived, in_hbm(coefficient), in_hbm(observed), in_hbm(kernel))
    returned = exchange(outgoing, devices, params, cells)
    gradient = pl.pallas_call(
        sum_kernel,
        out_shape=shape((params, tiles, cells), f32),
        in_specs=[VMEM, VMEM],
        out_specs=HBM,
        scratch_shapes=[
            pltpu.VMEM((messages, cells), f32),
            pltpu.VMEM((params, tiles, cells), f32),
            pltpu.SemaphoreType.DMA((params,)),
        ],
        compiler_params=pltpu.CompilerParams(vmem_limit_bytes=16 * MIB),
        name="add",
    )(requests, returned)
    return residual, gradient[None]


def solution(mesh):
    return jax.shard_map(
        per_device,
        mesh=mesh,
        in_specs=(
            P(AXES, None, None),
            P(AXES, None),
            P(AXES, None),
            P(AXES, None),
            P(AXES),
            P(AXES),
            P(AXES, None, None, None),
        ),
        out_specs=(P(AXES, None), P(AXES, None, None, None)),
        check_vma=False,
    )
```
